256 devices in a mesh: section: 4 (over x), tp: 16 (over y, z_hi, core), dp: 4 (over z_lo).
Axes of the slice: x: 4, y: 4, z: 8 (z_hi: 2, z_lo: 4; z = z_hi * 4 + z_lo), core: 2. Of those that a mesh axis runs over, the one named last changes fastest.
Arguments:
- responses: bfloat16 [2048, 8192], P(('section', 'tp'), 'dp'), may hold values from -6 to 6
- weights: bfloat16 [4, 8192, 16384], P('section', 'dp', 'tp'), may hold values from -0.0625 to 0.0625
- readout: float32 [4, 16384], P('section', 'tp'), may hold values from -0.09375 to 0.09375
- lengths: int32 [16], replicated, may hold values from 1 to 256, 2048 in all
- groups: int32 [16], replicated, may hold values from 0 to 3
Outputs:
- weight_grad: bfloat16 [4, 2048, 16384], P('dp', 'section', 'tp')
- policy_loss: float32 [], replicated
The draws below stay inside these ranges and needn't reach their ends.
Inputs may be any that keep to these rules, and one draw needn't show every extreme that they name: The lengths add up to 2048; the longest response has exactly 256 tokens.
All inputs are finite; a program needn't handle non-finite values.
Results may differ from the reference program's by a relative error of at most 0.005.
Values may be sent and summed in bfloat16 or wider, within the bound.
A program may use at most 64 MiB of HBM per device.

```python
import math
import jax
import jax.numpy as jnp
import numpy as np
from jax import lax

D = 8192
FF = 16384
RESP = 16
GROUPS = 4
TOKENS = 2048
MOST = 256
N_SECTION = 4
N_DP = 4


def plant(drawn, key, smallest, high):
    extent = drawn.shape
    index_at = [jax.random.randint(jax.random.fold_in(key, axis), (), 0, extent[axis]) for axis in range(len(extent))]
    drawn = drawn.at[tuple(index_at)].set(smallest)
    longest = extent.index(max(extent))
    index_at[longest] = (index_at[longest] + 1) % extent[longest]
    return drawn.at[tuple(index_at)].set(high)


def levels(own_key, shape, cuts, low, top_value):
    level, own = 1.0, jax.random.fold_in(own_key, 6)
    for axis_at, shards_of in cuts:
        steps = jnp.exp(jax.random.uniform(jax.random.fold_in(own, axis_at), (shards_of,), jnp.float32, low / len(cuts), top_value / len(cuts)))
        level = level * jnp.repeat(steps, shape[axis_at] // shards_of).reshape([-1 if axis == axis_at else 1 for axis in range(len(shape))])
    return level


def profile(amount, total, bound, slope):
    portions = [(1 << 20) // math.isqrt(standing ** slope) + 1 for standing in range(2, amount + 1)]
    rest, given = total - bound - (amount - 1), [1] * (amount - 1)
    while rest > 0:
        movable = [i for i in range(amount - 1) if given[i] < bound]
        pool, remaining = sum([portions[i] for i in movable]), rest
        for i in movable:
            extra = min(bound - given[i], max(1, remaining * portions[i] // pool), rest)
            given[i] = given[i] + extra
            rest = rest - extra
    return np.array([bound] + given)


def ragged_sizes(rng, count, total, reach, slope):
    if count == 2:
        one = jax.random.randint(rng, (), max(1, total - reach), min(reach, total - 1) + 1)
        return jnp.stack([one, total - one])
    tallies = jnp.asarray(profile(count, total, reach, slope), jnp.int32)
    pairs = (count - 1) // 2
    donor, receiver = tallies[1:1 + 2 * pairs:2], tallies[2:2 + 2 * pairs:2]
    room = jnp.minimum(donor - 1, reach - receiver)
    passed = jax.random.randint(jax.random.fold_in(rng, 1), (pairs,), 0, 1 << 20) % (room + 1)
    tallies = tallies.at[1:1 + 2 * pairs:2].set(donor - passed).at[2:2 + 2 * pairs:2].set(receiver + passed)
    return tallies[jax.random.permutation(jax.random.fold_in(rng, 2), count)]


def normal_values(own_key, shape, scale, limit, shards=(), held_as=jnp.bfloat16):
    result = scale * jax.random.normal(own_key, shape, jnp.float32)
    if shards:
        result = result * levels(own_key, shape, shards, -0.22, 0.18)
    return jnp.clip(result, -limit, limit).astype(held_as)


def setup_inputs(seed: int = 0) -> dict:
    splits = jax.random.split(jax.random.key(seed), 6)
    responses = normal_values(splits[0], (TOKENS, D), 1.0, 6.0, ((0, 64), (1, 4)))
    weights = normal_values(splits[1], (N_SECTION, D, FF), D ** -0.5, 0.0625, ((0, 4), (1, 4), (2, 16)))
    readout = normal_values(splits[2], (N_SECTION, FF), (FF // 4) ** -0.5, 0.09375, ((0, 4), (1, 16)), jnp.float32)
    lengths = ragged_sizes(splits[3], RESP, TOKENS, MOST, 2).astype(jnp.int32)
    groups = plant(jax.random.randint(splits[4], (RESP,), 0, GROUPS), jax.random.fold_in(splits[4], 1), 0, GROUPS - 1).astype(jnp.int32)
    return {"responses": responses, "weights": weights, "readout": readout, "lengths": lengths, "groups": groups}


kl_weight = 0.2

def advantages(rewards, groups):
    same_group = (groups[:, None] == groups[None, :]).astype(jnp.float32)
    members = lax.optimization_barrier(jnp.sum(same_group, axis=1))
    group_mean = lax.optimization_barrier(jnp.sum(same_group * rewards[None, :], axis=1)) / members
    spread = lax.optimization_barrier(jnp.sum(same_group * (rewards[None, :] - group_mean[:, None]) ** 2, axis=1)) / members
    return (rewards - group_mean) / jnp.sqrt(spread + 1.0)

def reference(responses, weights, readout, lengths, groups):
    scores = []
    learner_hidden = None
    for model in range(4):
        hidden = jnp.dot(responses, weights[model], preferred_element_type=jnp.float32)
        scores.append(lax.optimization_barrier(jnp.sum(jax.nn.silu(hidden) * readout[model][None, :], axis=1)))
        learner_hidden = hidden
    total_rows = responses.shape[0]
    position = jnp.arange(total_rows, dtype=jnp.int32)
    starts = (jnp.cumsum(lengths) - lengths).astype(jnp.int32)
    finish = (starts + lengths).astype(jnp.int32)
    in_response = ((position[:, None] >= starts[None, :]) & (position[:, None] < finish[None, :])).astype(jnp.float32)
    last_token = (position[:, None] == finish[None, :] - 1).astype(jnp.float32)
    token_len = lax.optimization_barrier(jnp.sum(in_response * lengths.astype(jnp.float32)[None, :], axis=1))
    rewards = lax.optimization_barrier(jnp.sum(last_token * scores[2][:, None], axis=0))
    advantage = advantages(rewards, groups)
    token_adv = lax.optimization_barrier(jnp.sum(in_response * advantage[None, :], axis=1))
    lp_old = jax.nn.log_sigmoid(scores[0])
    lp_ref = jax.nn.log_sigmoid(scores[1])
    lp_new = jax.nn.log_sigmoid(scores[3])
    prob_ratio = jnp.exp(lp_new - lp_old)
    log_gap = lp_ref - lp_new
    token_loss = -prob_ratio * token_adv + kl_weight * (jnp.exp(log_gap) - log_gap - 1.0)
    policy_loss = jnp.sum(token_loss / token_len) / RESP
    coeff = total_rows / (RESP * token_len) * (-prob_ratio * token_adv + kl_weight * (1.0 - jnp.exp(log_gap))) * jax.nn.sigmoid(-scores[3])
    sigmoid_z = jax.nn.sigmoid(learner_hidden)
    silu_slope = sigmoid_z * (1.0 + learner_hidden * (1.0 - sigmoid_z))
    hidden_grad = (coeff[:, None] * readout[3][None, :] * silu_slope).astype(jnp.bfloat16)
    weight_grad = jnp.dot(responses.T, hidden_grad, preferred_element_type=jnp.float32).astype(jnp.bfloat16)
    return (weight_grad.reshape(N_DP, D // N_DP, FF), policy_loss)
```

```python
import functools

import jax
import jax.numpy as jnp
from jax import lax
from jax.experimental import pallas as pl
from jax.experimental.pallas import tpu as pltpu
from jax.sharding import PartitionSpec as P

kl_weight = 0.2

RING = 4
SLOTS = 8
ROWS = 256
HALF = 128
SUB = 64
PIECE = 32
LAST = 3
Y_OFF = (0, 0, 3, 1, 3, 1, 2, 2)
H_OFF = (0, 1, 0, 0, 1, 1, 0, 1)


def wait_for(ref, sem):
    pltpu.make_async_copy(ref, ref, sem).wait()


def rows_at(start, size, step):
    return pl.ds(pl.multiple_of(start, step), size)


def slab_kernel(
    x_hbm, w_hbm, read_ref,
    score_ref, slope_out, feat_out,
    xg, wv, part_sum, landed, slope, lanes, score_rows, mine, peers, total, scores,
    local_sem, out_sem, gather_send, h_recv, x_recv, y_recv, sib_recv,
    sum_send, sum_recv, scat_send, scat_recv, line_send, line_recv,
    ring_send, ring_recv, peer_send, peer_recv, score_send, score_recv,
):
    sec = lax.axis_index("section")
    tp = lax.axis_index("tp")
    d = lax.axis_index("dp")
    y = tp // 4
    h = lax.rem(tp // 2, 2)
    c = lax.rem(tp, 2)

    def tp_at(y_, h_, c_):
        return (y_ * 2 + h_) * 2 + c_

    def ring(at, by):
        return lax.rem(at + by, RING)

    right, left = ring(sec, 1), ring(sec, 3)
    up, down = tp_at(ring(y, 1), h, c), tp_at(ring(y, 3), h, c)
    sibling = tp_at(y, h, 1 - c)
    far = tp_at(y, 1 - h, c)

    load_w = pltpu.make_async_copy(w_hbm.at[0], wv, local_sem.at[0])
    load_w.start()

    barrier = pltpu.get_barrier_semaphore()
    for k in range(1, 16):
        pl.semaphore_signal(
            barrier, inc=1,
            device_id={"section": sec, "tp": lax.rem(tp + k, 16), "dp": d},
            device_id_type=pl.DeviceIdType.MESH,
        )
    for k in range(1, 16):
        pl.semaphore_signal(
            barrier, inc=1,
            device_id={"section": ring(sec, k // 4), "tp": tp, "dp": ring(d, k % 4)},
            device_id_type=pl.DeviceIdType.MESH,
        )
    pl.semaphore_wait(barrier, 30)

    def push(src, dst, send_sem, recv_sem, sec_=None, tp_=None, d_=None):
        pltpu.make_async_remote_copy(
            src_ref=src, dst_ref=dst, send_sem=send_sem, recv_sem=recv_sem,
            device_id={
                "section": sec if sec_ is None else sec_,
                "tp": tp if tp_ is None else tp_,
                "dp": d if d_ is None else d_,
            },
            device_id_type=pl.DeviceIdType.MESH,
        ).start()

    origin = (sec, left, right, ring(sec, 2))

    def piece(slot, p, core):
        return xg.at[rows_at(slot * ROWS + origin[p] * SUB + core * PIECE, PIECE, PIECE)]

    def send_piece(src, slot, p, recv_sem, **to):
        push(src, piece(slot, p, c), gather_send, recv_sem, **to)

    def spread(slot, p, src):
        send_piece(src, (2, 4)[slot], p, y_recv.at[(2, 4)[slot], p], tp_=up)
        send_piece(src, (3, 5)[slot], p, y_recv.at[(3, 5)[slot], p], tp_=down)
        send_piece(src, slot, p, sib_recv.at[slot, p], tp_=sibling)

    own = pltpu.make_async_copy(x_hbm, piece(0, 0, c), local_sem.at[1])
    own.start()
    send_piece(x_hbm, 0, 0, x_recv.at[0, 0], sec_=right)
    send_piece(x_hbm, 0, 0, x_recv.at[0, 1], sec_=left)
    send_piece(x_hbm, 1, 0, h_recv, tp_=far)
    spread(0, 0, x_hbm)

    wait_for(piece(0, 1, c), x_recv.at[0, 0])
    send_piece(piece(0, 1, c), 0, 1, x_recv.at[0, 2], sec_=right)
    spread(0, 1, piece(0, 1, c))
    wait_for(piece(0, 2, c), x_recv.at[0, 1])
    spread(0, 2, piece(0, 2, c))
    wait_for(piece(0, 3, c), x_recv.at[0, 2])
    spread(0, 3, piece(0, 3, c))
    own.wait()
    load_w.wait()

    def second_block():
        wait_for(piece(1, 0, c), h_recv)
        send_piece(piece(1, 0, c), 1, 0, x_recv.at[1, 0], sec_=right)
        send_piece(piece(1, 0, c), 1, 0, x_recv.at[1, 1], sec_=left)
        spread(1, 0, piece(1, 0, c))
        wait_for(piece(1, 2, c), x_recv.at[1, 1])
        send_piece(piece(1, 2, c), 1, 2, x_recv.at[1, 2], sec_=left)
        spread(1, 2, piece(1, 2, c))
        wait_for(piece(1, 1, c), x_recv.at[1, 0])
        spread(1, 1, piece(1, 1, c))
        wait_for(piece(1, 3, c), x_recv.at[1, 2])
        spread(1, 3, piece(1, 3, c))

    def later_block(slot):
        for p in range(RING):
            wait_for(piece(slot, p, c), y_recv.at[slot, p])
            send_piece(piece(slot, p, c), slot, p, sib_recv.at[slot, p], tp_=sibling)

            @pl.when(slot == 2)
            def _():
                send_piece(piece(2, p, c), 6, p, y_recv.at[6, p], tp_=up)

            @pl.when(slot == 5)
            def _():
                send_piece(piece(5, p, c), 7, p, y_recv.at[7, p], tp_=down)

    def project(slot):
        for p in range(RING):
            wait_for(piece(slot, p, 1 - c), sib_recv.at[slot, p])
        block = rows_at(slot * ROWS, ROWS, ROWS)
        pltpu.make_async_copy(
            xg.at[block, rows_at(sec * 512, 512, 128)], feat_out.at[block], out_sem.at[0]
        ).start()
        for n in range(0, wv.shape[1], 256):
            part_sum[block, n:n + 256] = jnp.dot(
                xg[block, :], wv[:, n:n + 256], preferred_element_type=jnp.float32
            )

    def finish(start, slot, a):
        def some(t, carry):
            at = rows_at(start + t * 16, 16, 16)
            hidden = part_sum[at, :] + landed[at, :]
            gate = jax.nn.sigmoid(hidden)
            term = hidden * gate * read_ref[...]
            folded = term[:, 0:128]
            for n in range(128, term.shape[1], 128):
                folded = folded + term[:, n:n + 128]
            lanes[rows_at(a * SUB + t * 16, 16, 16), :] = folded

            @pl.when(sec == LAST)
            def _():
                slope[at, :] = (
                    read_ref[...] * gate * (1.0 + hidden * (1.0 - gate))
                ).astype(jnp.bfloat16)

            return carry

        lax.fori_loop(0, SUB // 16, some, 0)
        if a == 1:
            score_rows[pl.ds(slot, 1), :] = jnp.sum(
                jnp.transpose(lanes[...]), axis=0, keepdims=True
            )

    def add_up(i, half, a):
        hop = d if half == 1 else LAST - d
        onward = d + 1 if half == 1 else d - 1
        slot = i - hop
        start = slot * ROWS + half * HALF + a * SUB

        @pl.when((slot >= 0) & (slot < SLOTS))
        def _():
            at = rows_at(start, SUB, SUB)
            count = slot * 2 + a

            @pl.when(hop > 0)
            def _():
                wait_for(landed.at[at], sum_recv.at[half, count])

            @pl.when((hop > 0) & (hop < LAST))
            def _():
                part_sum[at, :] = part_sum[at, :] + landed[at, :]

            @pl.when(hop < LAST)
            def _():
                push(
                    part_sum.at[at], landed.at[at], sum_send.at[half],
                    sum_recv.at[half, count], d_=onward,
                )

            @pl.when(hop == LAST)
            def _():
                finish(start, slot, a)

    def quarter(slot, half, q):
        return slope.at[rows_at(slot * ROWS + half * HALF + q * PIECE, PIECE, PIECE)]

    def in_range(slot):
        return (slot >= 0) & (slot < SLOTS)

    def hand_on(i, half):
        hop = d if half == 0 else LAST - d
        onward = d + 1 if half == 0 else d - 1
        source = (hop == 0) & (sec == LAST)
        no_right = (hop == 0) & (sec == LAST - 1)
        no_left = (hop == 0) & (sec == 0)

        fresh = i - 3

        @pl.when(source & in_range(fresh))
        def _():
            for q in range(LAST):
                push(
                    quarter(fresh, half, q), quarter(fresh, half, q),
                    scat_send.at[half], scat_recv.at[half, fresh], sec_=q,
                )

        slot = i - 4 - hop

        @pl.when(in_range(slot))
        def _():
            held = quarter(slot, half, sec)

            @pl.when((hop == 0) & (sec < LAST))
            def _():
                wait_for(held, scat_recv.at[half, slot])

            @pl.when(hop > 0)
            def _():
                wait_for(held, line_recv.at[half, slot])

            @pl.when(hop < LAST)
            def _():
                push(held, held, line_send.at[half], line_recv.at[half, slot], d_=onward)

            @pl.when(jnp.logical_not(no_right))
            def _():
                push(held, held, ring_send.at[half], ring_recv.at[half, slot, 0], sec_=right)

            @pl.when(jnp.logical_not(no_left))
            def _():
                push(held, held, ring_send.at[half], ring_recv.at[half, slot, 1], sec_=left)

        slot1 = i - 5 - hop

        @pl.when(in_range(slot1))
        def _():
            from_left = quarter(slot1, half, left)
            from_right = quarter(slot1, half, right)

            @pl.when(jnp.logical_not(source))
            def _():
                wait_for(from_left, ring_recv.at[half, slot1, 0])
                wait_for(from_right, ring_recv.at[half, slot1, 1])

            if half == 0:
                @pl.when(jnp.logical_not(no_right))
                def _():
                    push(
                        from_left, from_left, ring_send.at[half],
                        ring_recv.at[half, slot1, 2], sec_=right,
                    )
            else:
                @pl.when(jnp.logical_not(no_left))
                def _():
                    push(
                        from_right, from_right, ring_send.at[half],
                        ring_recv.at[half, slot1, 2], sec_=left,
                    )

        slot2 = i - 6 - hop

        @pl.when(in_range(slot2))
        def _():
            @pl.when(jnp.logical_not(source))
            def _():
                wait_for(quarter(slot2, half, origin[3]), ring_recv.at[half, slot2, 2])

            at = rows_at(slot2 * ROWS + half * HALF, HALF, HALF)
            pltpu.make_async_copy(slope.at[at], slope_out.at[at], out_sem.at[1]).start()

    is_end = (d == 0) | (d == LAST)
    which = d // LAST

    def share_terms():
        for slot in range(SLOTS):
            row = ring(y, Y_OFF[slot]) * 2 + lax.rem(h + H_OFF[slot], 2)
            mine[pl.ds(row, 1), :] = score_rows[slot:slot + 1, :]
        for k in range(1, 16):
            push(mine, peers.at[tp], peer_send, peer_recv, tp_=lax.rem(tp + k, 16))
        peers[tp] = mine[...]

    def share_scores():
        wait_for(scores_like_peers(15), peer_recv)
        summed = peers[0]
        for k in range(1, 16):
            summed = summed + peers[k]
        total[...] = summed
        for k in range(1, 16):
            push(
                total, scores.at[sec * 2 + which], score_send, score_recv,
                sec_=ring(sec, k // 4), d_=ring(d, k % 4),
            )
        scores[sec * 2 + which] = summed

    def scores_like_peers(n):
        return peers.at[0:n]

    def step(i, carry):
        @pl.when(i < SLOTS)
        def _():
            project(i)

        for a in range(2):
            add_up(i, 1, a)
            add_up(i, 0, a)

        @pl.when(i == 0)
        def _():
            second_block()

        @pl.when((i >= 1) & (i < SLOTS - 1))
        def _():
            later_block(i + 1)

        @pl.when((i == 10) & is_end)
        def _():
            share_terms()

        hand_on(i, 0)
        hand_on(i, 1)

        @pl.when((i == 12) & is_end)
        def _():
            share_scores()

        return carry

    lax.fori_loop(0, SLOTS + 9, step, 0)

    @pl.when(is_end)
    def _():
        wait_for(scores.at[0:7], score_recv)

    @pl.when(jnp.logical_not(is_end))
    def _():
        wait_for(scores.at[0:8], score_recv)

    score_ref[...] = scores[...]

    wait_for(xg.at[0:63 * PIECE], gather_send)
    for half in range(2):
        sum_hop = d if half == 1 else LAST - d
        hop = d if half == 0 else LAST - d
        source = (hop == 0) & (sec == LAST)
        one = (hop == 0) & (sec == (LAST - 1 if half == 0 else 0))
        two = (hop == 0) & (sec == (0 if half == 0 else LAST - 1))

        @pl.when(sum_hop < LAST)
        def _():
            wait_for(part_sum.at[0:SLOTS * HALF], sum_send.at[half])

        @pl.when(source)
        def _():
            wait_for(slope.at[0:3 * SLOTS * PIECE], scat_send.at[half])

        @pl.when(hop < LAST)
        def _():
            wait_for(slope.at[0:SLOTS * PIECE], line_send.at[half])

        @pl.when(one)
        def _():
            wait_for(slope.at[0:SLOTS * PIECE], ring_send.at[half])

        @pl.when(two)
        def _():
            wait_for(slope.at[0:2 * SLOTS * PIECE], ring_send.at[half])

        @pl.when(jnp.logical_not(one | two))
        def _():
            wait_for(slope.at[0:3 * SLOTS * PIECE], ring_send.at[half])

    @pl.when(is_end)
    def _():
        wait_for(scores_like_peers(15), peer_send)
        wait_for(scores_like_peers(15), score_send)

    wait_for(feat_out, out_sem.at[0])
    wait_for(slope_out, out_sem.at[1])


def score_and_slope(responses, weights, readout):
    tokens, width, units = ROWS * SLOTS, weights.shape[1], weights.shape[2]
    block_width = width // RING
    dma = pltpu.SemaphoreType.DMA
    any_space = pl.BlockSpec(memory_space=pl.ANY)
    in_vmem = pl.BlockSpec(memory_space=pltpu.VMEM)
    return pl.pallas_call(
        slab_kernel,
        out_shape=(
            jax.ShapeDtypeStruct((8, 8, 128), jnp.float32),
            jax.ShapeDtypeStruct((tokens, units), jnp.bfloat16),
            jax.ShapeDtypeStruct((tokens, block_width), jnp.bfloat16),
        ),
        in_specs=[any_space, any_space, in_vmem],
        out_specs=(in_vmem, any_space, any_space),
        scratch_shapes=[
            pltpu.VMEM((tokens, width), jnp.bfloat16),
            pltpu.VMEM((width, units), jnp.bfloat16),
            pltpu.VMEM((tokens, units), jnp.float32),
            pltpu.VMEM((tokens, units), jnp.float32),
            pltpu.VMEM((tokens, units), jnp.bfloat16),
            pltpu.VMEM((128, 128), jnp.float32),
            pltpu.VMEM((8, 128), jnp.float32),
            pltpu.VMEM((8, 128), jnp.float32),
            pltpu.VMEM((16, 8, 128), jnp.float32),
            pltpu.VMEM((8, 128), jnp.float32),
            pltpu.VMEM((8, 8, 128), jnp.float32),
            dma((2,)), dma((2,)), dma, dma, dma((2, 3)), dma((8, 4)), dma((8, 4)),
            dma((2,)), dma((2, 16)), dma((2,)), dma((2, 8)), dma((2,)), dma((2, 8)),
            dma((2,)), dma((2, 8, 3)), dma, dma, dma, dma,
        ],
        compiler_params=pltpu.CompilerParams(
            collective_id=0, has_side_effects=True, vmem_limit_bytes=50 * 1024 * 1024,
        ),
        name="score_and_slope",
    )(responses, weights, readout)


def advantages(rewards, groups):
    same_group = (groups[:, None] == groups[None, :]).astype(jnp.float32)
    members = jnp.sum(same_group, axis=1)
    group_mean = jnp.sum(same_group * rewards[None, :], axis=1) / members
    spread = jnp.sum(same_group * (rewards[None, :] - group_mean[:, None]) ** 2, axis=1) / members
    return (rewards - group_mean) / jnp.sqrt(spread + 1.0)


def contract_rows(left, right):
    return lax.dot_general(
        left, right, (((0,), (0,)), ((), ())), preferred_element_type=jnp.float32
    )


def local(responses, weights, readout, lengths, groups):
    scores, slope, features = score_and_slope(responses, weights, readout)
    total_rows = slope.shape[0]
    resp_count = lengths.shape[0]
    joined = scores.reshape(RING, total_rows)
    shape = (2, 4, 2, 2, SUB)
    half, at_y, at_h, at_x, inner = (
        lax.broadcasted_iota(jnp.int32, shape, n) for n in range(5)
    )
    position = (((half * 2 + at_x) * 4 + at_y) * 2 + at_h) * SUB + inner
    position = position.reshape(total_rows)
    starts = jnp.cumsum(lengths) - lengths
    finish = starts + lengths
    in_response = (
        (position[:, None] >= starts[None, :]) & (position[:, None] < finish[None, :])
    ).astype(jnp.float32)
    last_token = (position[:, None] == finish[None, :] - 1).astype(jnp.float32)
    token_len = jnp.sum(in_response * lengths.astype(jnp.float32)[None, :], axis=1)
    lp_old = jax.nn.log_sigmoid(joined[0])
    lp_ref = jax.nn.log_sigmoid(joined[1])
    lp_new = jax.nn.log_sigmoid(joined[3])
    prob_ratio = jnp.exp(lp_new - lp_old)
    log_gap = lp_ref - lp_new
    penalty = kl_weight * (jnp.exp(log_gap) - log_gap - 1.0)
    rewards = jnp.sum(last_token * joined[2][:, None], axis=0)
    advantage = advantages(rewards, groups)
    token_adv = jnp.sum(in_response * advantage[None, :], axis=1)
    token_loss = -prob_ratio * token_adv + penalty
    policy_loss = jnp.sum(token_loss / token_len) / resp_count
    coeff = (
        total_rows
        / (resp_count * token_len)
        * (-prob_ratio * token_adv + kl_weight * (1.0 - jnp.exp(log_gap)))
        * jax.nn.sigmoid(-joined[3])
    )
    tp = lax.axis_index("tp")
    block = (
        lax.rem(tp // 4 + jnp.array(Y_OFF, jnp.int32), 4) * 2
        + lax.rem(tp // 2 + jnp.array(H_OFF, jnp.int32), 2)
    )
    by_block = coeff.reshape(2, SLOTS, HALF).transpose(1, 0, 2).reshape(SLOTS, ROWS)
    ordered = jnp.take(by_block, block, axis=0).reshape(total_rows)
    hidden_grad = ordered[:, None] * slope.astype(jnp.float32)
    upper = hidden_grad.astype(jnp.bfloat16)
    lower = (hidden_grad - upper.astype(jnp.float32)).astype(jnp.bfloat16)
    weight_grad = contract_rows(features, upper) + contract_rows(features, lower)
    return (weight_grad.astype(jnp.bfloat16)[None], policy_loss)


def solution(mesh):
    return jax.shard_map(
        local,
        mesh=mesh,
        in_specs=(
            P(("section", "tp"), "dp"),
            P("section", "dp", "tp"),
            P("section", "tp"),
            P(),
            P(),
        ),
        out_specs=(P("dp", "section", "tp"), P()),
        check_vma=False,
    )
```

```python
import functools

import jax
import jax.numpy as jnp
from jax import lax
from jax.experimental import pallas as pl
from jax.experimental.pallas import tpu as pltpu
from jax.sharding import PartitionSpec as P

kl_weight = 0.2

RING = 4
SLOTS = 8
ROWS = 256
HALF = 128
SUB = 64
PIECE = 32
LAST = 3
STEPS = 32767.0
Y_OFF = (0, 0, 3, 1, 3, 1, 2, 2)
H_OFF = (0, 1, 0, 0, 1, 1, 0, 1)


def wait_for(ref, sem):
    pltpu.make_async_copy(ref, ref, sem).wait()


def rows_at(start, size, step):
    return pl.ds(pl.multiple_of(start, step), size)


def slab_kernel(
    x_hbm, w_hbm, read_ref,
    score_ref, slope_out, feat_out,
    xg, wv, part_sum, sent, landed, unit_sent, unit_landed, slope, lanes, score_rows, mine, peers, total, scores,
    local_sem, out_sem, gather_send, h_recv, x_recv, y_recv, sib_recv,
    sum_send, sum_recv, unit_send, unit_recv, scat_send, scat_recv, line_send, line_recv,
    ring_send, ring_recv, peer_send, peer_recv, score_send, score_recv,
):
    sec = lax.axis_index("section")
    tp = lax.axis_index("tp")
    d = lax.axis_index("dp")
    y = tp // 4
    h = lax.rem(tp // 2, 2)
    c = lax.rem(tp, 2)

    def tp_at(y_, h_, c_):
        return (y_ * 2 + h_) * 2 + c_

    def ring(at, by):
        return lax.rem(at + by, RING)

    right, left = ring(sec, 1), ring(sec, 3)
    up, down = tp_at(ring(y, 1), h, c), tp_at(ring(y, 3), h, c)
    sibling = tp_at(y, h, 1 - c)
    far = tp_at(y, 1 - h, c)

    load_w = pltpu.make_async_copy(w_hbm.at[0], wv, local_sem.at[0])
    load_w.start()

    barrier = pltpu.get_barrier_semaphore()
    for k in range(1, 16):
        pl.semaphore_signal(
            barrier, inc=1,
            device_id={"section": sec, "tp": lax.rem(tp + k, 16), "dp": d},
            device_id_type=pl.DeviceIdType.MESH,
        )
    for k in range(1, 16):
        pl.semaphore_signal(
            barrier, inc=1,
            device_id={"section": ring(sec, k // 4), "tp": tp, "dp": ring(d, k % 4)},
            device_id_type=pl.DeviceIdType.MESH,
        )
    pl.semaphore_wait(barrier, 30)

    def push(src, dst, send_sem, recv_sem, sec_=None, tp_=None, d_=None):
        pltpu.make_async_remote_copy(
            src_ref=src, dst_ref=dst, send_sem=send_sem, recv_sem=recv_sem,
            device_id={
                "section": sec if sec_ is None else sec_,
                "tp": tp if tp_ is None else tp_,
                "dp": d if d_ is None else d_,
            },
            device_id_type=pl.DeviceIdType.MESH,
        ).start()

    origin = (sec, left, right, ring(sec, 2))

    def piece(slot, p, core):
        return xg.at[rows_at(slot * ROWS + origin[p] * SUB + core * PIECE, PIECE, PIECE)]

    def send_piece(src, slot, p, recv_sem, **to):
        push(src, piece(slot, p, c), gather_send, recv_sem, **to)

    def spread(slot, p, src):
        send_piece(src, (2, 4)[slot], p, y_recv.at[(2, 4)[slot], p], tp_=up)
        send_piece(src, (3, 5)[slot], p, y_recv.at[(3, 5)[slot], p], tp_=down)
        send_piece(src, slot, p, sib_recv.at[slot, p], tp_=sibling)

    own = pltpu.make_async_copy(x_hbm, piece(0, 0, c), local_sem.at[1])
    own.start()
    send_piece(x_hbm, 0, 0, x_recv.at[0, 0], sec_=right)
    send_piece(x_hbm, 0, 0, x_recv.at[0, 1], sec_=left)
    send_piece(x_hbm, 1, 0, h_recv, tp_=far)
    spread(0, 0, x_hbm)

    wait_for(piece(0, 1, c), x_recv.at[0, 0])
    send_piece(piece(0, 1, c), 0, 1, x_recv.at[0, 2], sec_=right)
    spread(0, 1, piece(0, 1, c))
    wait_for(piece(0, 2, c), x_recv.at[0, 1])
    spread(0, 2, piece(0, 2, c))
    wait_for(piece(0, 3, c), x_recv.at[0, 2])
    spread(0, 3, piece(0, 3, c))
    own.wait()
    load_w.wait()

    def second_block():
        wait_for(piece(1, 0, c), h_recv)
        send_piece(piece(1, 0, c), 1, 0, x_recv.at[1, 0], sec_=right)
        send_piece(piece(1, 0, c), 1, 0, x_recv.at[1, 1], sec_=left)
        spread(1, 0, piece(1, 0, c))
        wait_for(piece(1, 2, c), x_recv.at[1, 1])
        send_piece(piece(1, 2, c), 1, 2, x_recv.at[1, 2], sec_=left)
        spread(1, 2, piece(1, 2, c))
        wait_for(piece(1, 1, c), x_recv.at[1, 0])
        spread(1, 1, piece(1, 1, c))
        wait_for(piece(1, 3, c), x_recv.at[1, 2])
        spread(1, 3, piece(1, 3, c))

    def later_block(slot):
        for p in range(RING):
            wait_for(piece(slot, p, c), y_recv.at[slot, p])
            send_piece(piece(slot, p, c), slot, p, sib_recv.at[slot, p], tp_=sibling)

            @pl.when(slot == 2)
            def _():
                send_piece(piece(2, p, c), 6, p, y_recv.at[6, p], tp_=up)

            @pl.when(slot == 5)
            def _():
                send_piece(piece(5, p, c), 7, p, y_recv.at[7, p], tp_=down)

    def project(slot):
        for p in range(RING):
            wait_for(piece(slot, p, 1 - c), sib_recv.at[slot, p])
        block = rows_at(slot * ROWS, ROWS, ROWS)
        pltpu.make_async_copy(
            xg.at[block, rows_at(sec * 512, 512, 128)], feat_out.at[block], out_sem.at[0]
        ).start()
        for n in range(0, wv.shape[1], 256):
            part_sum[block, n:n + 256] = jnp.dot(
                xg[block, :], wv[:, n:n + 256], preferred_element_type=jnp.float32
            )

    def decode(at, chunk, cols):
        count = landed[at, cols].astype(jnp.int32).astype(jnp.float32)
        return count * unit_landed[chunk, :, cols]

    def encode(at, chunk, add):
        for n in range(0, part_sum.shape[1], 256):
            cols = slice(n, n + 256)
            value = part_sum[at, cols]
            if add:
                value = value + decode(at, chunk, cols)
            most = jnp.max(jnp.abs(value), axis=0, keepdims=True)
            most = jnp.maximum(most, 1e-30)
            unit_sent[chunk, :, cols] = most * (1.0 / STEPS)
            count = jnp.round(value * (STEPS / most)).astype(jnp.int32)
            sent[at, cols] = count.astype(jnp.int16)

    def finish(start, slot, a, chunk):
        def some(t, carry):
            at = rows_at(start + t * 16, 16, 16)
            hidden = part_sum[at, :] + decode(at, chunk, slice(None))
            gate = jax.nn.sigmoid(hidden)
            term = hidden * gate * read_ref[...]
            folded = term[:, 0:128]
            for n in range(128, term.shape[1], 128):
                folded = folded + term[:, n:n + 128]
            lanes[rows_at(a * SUB + t * 16, 16, 16), :] = folded

            @pl.when(sec == LAST)
            def _():
                slope[at, :] = (
                    read_ref[...] * gate * (1.0 + hidden * (1.0 - gate))
                ).astype(jnp.bfloat16)

            return carry

        lax.fori_loop(0, SUB // 16, some, 0)
        if a == 1:
            score_rows[pl.ds(slot, 1), :] = jnp.sum(
                jnp.transpose(lanes[...]), axis=0, keepdims=True
            )

    def add_up(i, half, a):
        hop = d if half == 1 else LAST - d
        onward = d + 1 if half == 1 else d - 1
        slot = i - hop
        start = slot * ROWS + half * HALF + a * SUB

        @pl.when((slot >= 0) & (slot < SLOTS))
        def _():
            at = rows_at(start, SUB, SUB)
            count = slot * 2 + a
            chunk = slot * 4 + half * 2 + a

            @pl.when(hop > 0)
            def _():
                wait_for(landed.at[at], sum_recv.at[half, count])
                wait_for(unit_landed.at[chunk], unit_recv.at[half, count])

            @pl.when(hop == 0)
            def _():
                encode(at, chunk, False)

            @pl.when((hop > 0) & (hop < LAST))
            def _():
                encode(at, chunk, True)

            @pl.when(hop < LAST)
            def _():
                push(
                    sent.at[at], landed.at[at], sum_send.at[half],
                    sum_recv.at[half, count], d_=onward,
                )
                push(
                    unit_sent.at[chunk], unit_landed.at[chunk], unit_send.at[half],
                    unit_recv.at[half, count], d_=onward,
                )

            @pl.when(hop == LAST)
            def _():
                finish(start, slot, a, chunk)

    def quarter(slot, half, q):
        return slope.at[rows_at(slot * ROWS + half * HALF + q * PIECE, PIECE, PIECE)]

    def in_range(slot):
        return (slot >= 0) & (slot < SLOTS)

    def hand_on(i, half):
        hop = d if half == 0 else LAST - d
        onward = d + 1 if half == 0 else d - 1
        source = (hop == 0) & (sec == LAST)
        no_right = (hop == 0) & (sec == LAST - 1)
        no_left = (hop == 0) & (sec == 0)

        fresh = i - 3

        @pl.when(source & in_range(fresh))
        def _():
            for q in range(LAST):
                push(
                    quarter(fresh, half, q), quarter(fresh, half, q),
                    scat_send.at[half], scat_recv.at[half, fresh], sec_=q,
                )

        slot = i - 4 - hop

        @pl.when(in_range(slot))
        def _():
            held = quarter(slot, half, sec)

            @pl.when((hop == 0) & (sec < LAST))
            def _():
                wait_for(held, scat_recv.at[half, slot])

            @pl.when(hop > 0)
            def _():
                wait_for(held, line_recv.at[half, slot])

            @pl.when(hop < LAST)
            def _():
                push(held, held, line_send.at[half], line_recv.at[half, slot], d_=onward)

            @pl.when(jnp.logical_not(no_right))
            def _():
                push(held, held, ring_send.at[half], ring_recv.at[half, slot, 0], sec_=right)

            @pl.when(jnp.logical_not(no_left))
            def _():
                push(held, held, ring_send.at[half], ring_recv.at[half, slot, 1], sec_=left)

        slot1 = i - 5 - hop

        @pl.when(in_range(slot1))
        def _():
            from_left = quarter(slot1, half, left)
            from_right = quarter(slot1, half, right)

            @pl.when(jnp.logical_not(source))
            def _():
                wait_for(from_left, ring_recv.at[half, slot1, 0])
                wait_for(from_right, ring_recv.at[half, slot1, 1])

            if half == 0:
                @pl.when(jnp.logical_not(no_right))
                def _():
                    push(
                        from_left, from_left, ring_send.at[half],
                        ring_recv.at[half, slot1, 2], sec_=right,
                    )
            else:
                @pl.when(jnp.logical_not(no_left))
                def _():
                    push(
                        from_right, from_right, ring_send.at[half],
                        ring_recv.at[half, slot1, 2], sec_=left,
                    )

        slot2 = i - 6 - hop

        @pl.when(in_range(slot2))
        def _():
            @pl.when(jnp.logical_not(source))
            def _():
                wait_for(quarter(slot2, half, origin[3]), ring_recv.at[half, slot2, 2])

            at = rows_at(slot2 * ROWS + half * HALF, HALF, HALF)
            pltpu.make_async_copy(slope.at[at], slope_out.at[at], out_sem.at[1]).start()

    is_end = (d == 0) | (d == LAST)
    which = d // LAST

    def share_terms():
        for slot in range(SLOTS):
            row = ring(y, Y_OFF[slot]) * 2 + lax.rem(h + H_OFF[slot], 2)
            mine[pl.ds(row, 1), :] = score_rows[slot:slot + 1, :]
        for k in range(1, 16):
            push(mine, peers.at[tp], peer_send, peer_recv, tp_=lax.rem(tp + k, 16))
        peers[tp] = mine[...]

    def share_scores():
        wait_for(scores_like_peers(15), peer_recv)
        summed = peers[0]
        for k in range(1, 16):
            summed = summed + peers[k]
        total[...] = summed
        for k in range(1, 16):
            push(
                total, scores.at[sec * 2 + which], score_send, score_recv,
                sec_=ring(sec, k // 4), d_=ring(d, k % 4),
            )
        scores[sec * 2 + which] = summed

    def scores_like_peers(n):
        return peers.at[0:n]

    def step(i, carry):
        @pl.when(i < SLOTS)
        def _():
            project(i)

        for a in range(2):
            add_up(i, 1, a)
            add_up(i, 0, a)

        @pl.when(i == 0)
        def _():
            second_block()

        @pl.when((i >= 1) & (i < SLOTS - 1))
        def _():
            later_block(i + 1)

        @pl.when((i == 10) & is_end)
        def _():
            share_terms()

        hand_on(i, 0)
        hand_on(i, 1)

        @pl.when((i == 12) & is_end)
        def _():
            share_scores()

        return carry

    lax.fori_loop(0, SLOTS + 9, step, 0)

    @pl.when(is_end)
    def _():
        wait_for(scores.at[0:7], score_recv)

    @pl.when(jnp.logical_not(is_end))
    def _():
        wait_for(scores.at[0:8], score_recv)

    score_ref[...] = scores[...]

    wait_for(xg.at[0:63 * PIECE], gather_send)
    for half in range(2):
        sum_hop = d if half == 1 else LAST - d
        hop = d if half == 0 else LAST - d
        source = (hop == 0) & (sec == LAST)
        one = (hop == 0) & (sec == (LAST - 1 if half == 0 else 0))
        two = (hop == 0) & (sec == (0 if half == 0 else LAST - 1))

        @pl.when(sum_hop < LAST)
        def _():
            wait_for(sent.at[0:SLOTS * HALF], sum_send.at[half])
            wait_for(unit_sent.at[0:SLOTS * 2], unit_send.at[half])

        @pl.when(source)
        def _():
            wait_for(slope.at[0:3 * SLOTS * PIECE], scat_send.at[half])

        @pl.when(hop < LAST)
        def _():
            wait_for(slope.at[0:SLOTS * PIECE], line_send.at[half])

        @pl.when(one)
        def _():
            wait_for(slope.at[0:SLOTS * PIECE], ring_send.at[half])

        @pl.when(two)
        def _():
            wait_for(slope.at[0:2 * SLOTS * PIECE], ring_send.at[half])

        @pl.when(jnp.logical_not(one | two))
        def _():
            wait_for(slope.at[0:3 * SLOTS * PIECE], ring_send.at[half])

    @pl.when(is_end)
    def _():
        wait_for(scores_like_peers(15), peer_send)
        wait_for(scores_like_peers(15), score_send)

    wait_for(feat_out, out_sem.at[0])
    wait_for(slope_out, out_sem.at[1])


def score_and_slope(responses, weights, readout):
    tokens, width, units = ROWS * SLOTS, weights.shape[1], weights.shape[2]
    block_width = width // RING
    dma = pltpu.SemaphoreType.DMA
    any_space = pl.BlockSpec(memory_space=pl.ANY)
    in_vmem = pl.BlockSpec(memory_space=pltpu.VMEM)
    return pl.pallas_call(
        slab_kernel,
        out_shape=(
            jax.ShapeDtypeStruct((8, 8, 128), jnp.float32),
            jax.ShapeDtypeStruct((tokens, units), jnp.bfloat16),
            jax.ShapeDtypeStruct((tokens, block_width), jnp.bfloat16),
        ),
        in_specs=[any_space, any_space, in_vmem],
        out_specs=(in_vmem, any_space, any_space),
        scratch_shapes=[
            pltpu.VMEM((tokens, width), jnp.bfloat16),
            pltpu.VMEM((width, units), jnp.bfloat16),
            pltpu.VMEM((tokens, units), jnp.float32),
            pltpu.VMEM((tokens, units), jnp.int16),
            pltpu.VMEM((tokens, units), jnp.int16),
            pltpu.VMEM((4 * SLOTS, 1, units), jnp.float32),
            pltpu.VMEM((4 * SLOTS, 1, units), jnp.float32),
            pltpu.VMEM((tokens, units), jnp.bfloat16),
            pltpu.VMEM((128, 128), jnp.float32),
            pltpu.VMEM((8, 128), jnp.float32),
            pltpu.VMEM((8, 128), jnp.float32),
            pltpu.VMEM((16, 8, 128), jnp.float32),
            pltpu.VMEM((8, 128), jnp.float32),
            pltpu.VMEM((8, 8, 128), jnp.float32),
            dma((2,)), dma((2,)), dma, dma, dma((2, 3)), dma((8, 4)), dma((8, 4)),
            dma((2,)), dma((2, 16)), dma((2,)), dma((2, 16)), dma((2,)), dma((2, 8)), dma((2,)), dma((2, 8)),
            dma((2,)), dma((2, 8, 3)), dma, dma, dma, dma,
        ],
        compiler_params=pltpu.CompilerParams(
            collective_id=0, has_side_effects=True, vmem_limit_bytes=50 * 1024 * 1024,
        ),
        name="score_and_slope",
    )(responses, weights, readout)


def advantages(rewards, groups):
    same_group = (groups[:, None] == groups[None, :]).astype(jnp.float32)
    members = jnp.sum(same_group, axis=1)
    group_mean = jnp.sum(same_group * rewards[None, :], axis=1) / members
    spread = jnp.sum(same_group * (rewards[None, :] - group_mean[:, None]) ** 2, axis=1) / members
    return (rewards - group_mean) / jnp.sqrt(spread + 1.0)


def contract_rows(left, right):
    return lax.dot_general(
        left, right, (((0,), (0,)), ((), ())), preferred_element_type=jnp.float32
    )


def local(responses, weights, readout, lengths, groups):
    scores, slope, features = score_and_slope(responses, weights, readout)
    total_rows = slope.shape[0]
    resp_count = lengths.shape[0]
    joined = scores.reshape(RING, total_rows)
    shape = (2, 4, 2, 2, SUB)
    half, at_y, at_h, at_x, inner = (
        lax.broadcasted_iota(jnp.int32, shape, n) for n in range(5)
    )
    position = (((half * 2 + at_x) * 4 + at_y) * 2 + at_h) * SUB + inner
    position = position.reshape(total_rows)
    starts = jnp.cumsum(lengths) - lengths
    finish = starts + lengths
    in_response = (
        (position[:, None] >= starts[None, :]) & (position[:, None] < finish[None, :])
    ).astype(jnp.float32)
    last_token = (position[:, None] == finish[None, :] - 1).astype(jnp.float32)
    token_len = jnp.sum(in_response * lengths.astype(jnp.float32)[None, :], axis=1)
    lp_old = jax.nn.log_sigmoid(joined[0])
    lp_ref = jax.nn.log_sigmoid(joined[1])
    lp_new = jax.nn.log_sigmoid(joined[3])
    prob_ratio = jnp.exp(lp_new - lp_old)
    log_gap = lp_ref - lp_new
    penalty = kl_weight * (jnp.exp(log_gap) - log_gap - 1.0)
    rewards = jnp.sum(last_token * joined[2][:, None], axis=0)
    advantage = advantages(rewards, groups)
    token_adv = jnp.sum(in_response * advantage[None, :], axis=1)
    token_loss = -prob_ratio * token_adv + penalty
    policy_loss = jnp.sum(token_loss / token_len) / resp_count
    coeff = (
        total_rows
        / (resp_count * token_len)
        * (-prob_ratio * token_adv + kl_weight * (1.0 - jnp.exp(log_gap)))
        * jax.nn.sigmoid(-joined[3])
    )
    tp = lax.axis_index("tp")
    block = (
        lax.rem(tp // 4 + jnp.array(Y_OFF, jnp.int32), 4) * 2
        + lax.rem(tp // 2 + jnp.array(H_OFF, jnp.int32), 2)
    )
    by_block = coeff.reshape(2, SLOTS, HALF).transpose(1, 0, 2).reshape(SLOTS, ROWS)
    ordered = jnp.take(by_block, block, axis=0).reshape(total_rows)
    hidden_grad = ordered[:, None] * slope.astype(jnp.float32)
    upper = hidden_grad.astype(jnp.bfloat16)
    lower = (hidden_grad - upper.astype(jnp.float32)).astype(jnp.bfloat16)
    weight_grad = contract_rows(features, upper) + contract_rows(features, lower)
    return (weight_grad.astype(jnp.bfloat16)[None], policy_loss)


def solution(mesh):
    return jax.shard_map(
        local,
        mesh=mesh,
        in_specs=(
            P(("section", "tp"), "dp"),
            P("section", "dp", "tp"),
            P("section", "tp"),
            P(),
            P(),
        ),
        out_specs=(P("dp", "section", "tp"), P()),
        check_vma=False,
    )
```

```python
import functools

import jax
import jax.numpy as jnp
from jax import lax
from jax.experimental import pallas as pl
from jax.experimental.pallas import tpu as pltpu
from jax.sharding import PartitionSpec as P

kl_weight = 0.2

RING = 4
SLOTS = 8
ROWS = 256
HALF = 128
SUB = 64
PIECE = 32
LAST = 3
STEPS = 32767.0
Y_OFF = (0, 0, 3, 1, 3, 1, 2, 2)
H_OFF = (0, 1, 0, 0, 1, 1, 0, 1)


def wait_for(ref, sem):
    pltpu.make_async_copy(ref, ref, sem).wait()


def rows_at(start, size, step):
    return pl.ds(pl.multiple_of(start, step), size)


def slab_kernel(
    x_hbm, w_hbm, read_ref,
    score_ref, slope_out, feat_out,
    xg, wv, part_sum, sent, landed, unit_sent, unit_landed, slope, lanes, score_rows, mine, peers, total, scores,
    local_sem, out_sem, gather_send, h_recv, x_recv, y_recv, sib_recv,
    sum_send, sum_recv, unit_send, unit_recv, scat_send, scat_recv, line_send, line_recv,
    ring_send, ring_recv, peer_send, peer_recv, score_send, score_recv,
):
    sec = lax.axis_index("section")
    tp = lax.axis_index("tp")
    d = lax.axis_index("dp")
    y = tp // 4
    h = lax.rem(tp // 2, 2)
    c = lax.rem(tp, 2)

    def tp_at(y_, h_, c_):
        return (y_ * 2 + h_) * 2 + c_

    def ring(at, by):
        return lax.rem(at + by, RING)

    right, left = ring(sec, 1), ring(sec, 3)
    up, down = tp_at(ring(y, 1), h, c), tp_at(ring(y, 3), h, c)
    sibling = tp_at(y, h, 1 - c)
    far = tp_at(y, 1 - h, c)

    load_w = pltpu.make_async_copy(w_hbm.at[0], wv, local_sem.at[0])
    load_w.start()

    barrier = pltpu.get_barrier_semaphore()
    for k in range(1, 16):
        pl.semaphore_signal(
            barrier, inc=1,
            device_id={"section": sec, "tp": lax.rem(tp + k, 16), "dp": d},
            device_id_type=pl.DeviceIdType.MESH,
        )
    for k in range(1, 16):
        pl.semaphore_signal(
            barrier, inc=1,
            device_id={"section": ring(sec, k // 4), "tp": tp, "dp": ring(d, k % 4)},
            device_id_type=pl.DeviceIdType.MESH,
        )
    pl.semaphore_wait(barrier, 30)

    def push(src, dst, send_sem, recv_sem, sec_=None, tp_=None, d_=None):
        pltpu.make_async_remote_copy(
            src_ref=src, dst_ref=dst, send_sem=send_sem, recv_sem=recv_sem,
            device_id={
                "section": sec if sec_ is None else sec_,
                "tp": tp if tp_ is None else tp_,
                "dp": d if d_ is None else d_,
            },
            device_id_type=pl.DeviceIdType.MESH,
        ).start()

    origin = (sec, left, right, ring(sec, 2))

    def piece(slot, p, core):
        return xg.at[rows_at(slot * ROWS + origin[p] * SUB + core * PIECE, PIECE, PIECE)]

    def send_piece(src, slot, p, recv_sem, **to):
        push(src, piece(slot, p, c), gather_send, recv_sem, **to)

    def spread(slot, p, src):
        send_piece(src, (2, 4)[slot], p, y_recv.at[(2, 4)[slot], p], tp_=up)
        send_piece(src, (3, 5)[slot], p, y_recv.at[(3, 5)[slot], p], tp_=down)
        send_piece(src, slot, p, sib_recv.at[slot, p], tp_=sibling)

    own = pltpu.make_async_copy(x_hbm, piece(0, 0, c), local_sem.at[1])
    own.start()
    send_piece(x_hbm, 0, 0, x_recv.at[0, 0], sec_=right)
    send_piece(x_hbm, 0, 0, x_recv.at[0, 1], sec_=left)
    send_piece(x_hbm, 1, 0, h_recv, tp_=far)
    spread(0, 0, x_hbm)

    wait_for(piece(0, 1, c), x_recv.at[0, 0])
    send_piece(piece(0, 1, c), 0, 1, x_recv.at[0, 2], sec_=right)
    spread(0, 1, piece(0, 1, c))
    wait_for(piece(0, 2, c), x_recv.at[0, 1])
    spread(0, 2, piece(0, 2, c))
    wait_for(piece(0, 3, c), x_recv.at[0, 2])
    spread(0, 3, piece(0, 3, c))
    own.wait()
    load_w.wait()

    def second_block():
        wait_for(piece(1, 0, c), h_recv)
        send_piece(piece(1, 0, c), 1, 0, x_recv.at[1, 0], sec_=right)
        send_piece(piece(1, 0, c), 1, 0, x_recv.at[1, 1], sec_=left)
        spread(1, 0, piece(1, 0, c))
        wait_for(piece(1, 2, c), x_recv.at[1, 1])
        send_piece(piece(1, 2, c), 1, 2, x_recv.at[1, 2], sec_=left)
        spread(1, 2, piece(1, 2, c))
        wait_for(piece(1, 1, c), x_recv.at[1, 0])
        spread(1, 1, piece(1, 1, c))
        wait_for(piece(1, 3, c), x_recv.at[1, 2])
        spread(1, 3, piece(1, 3, c))

    def later_block(slot):
        for p in range(RING):
            wait_for(piece(slot, p, c), y_recv.at[slot, p])
            send_piece(piece(slot, p, c), slot, p, sib_recv.at[slot, p], tp_=sibling)

            @pl.when(slot == 2)
            def _():
                send_piece(piece(2, p, c), 6, p, y_recv.at[6, p], tp_=up)

            @pl.when(slot == 5)
            def _():
                send_piece(piece(5, p, c), 7, p, y_recv.at[7, p], tp_=down)

    def project(slot):
        for p in range(RING):
            wait_for(piece(slot, p, 1 - c), sib_recv.at[slot, p])
        block = rows_at(slot * ROWS, ROWS, ROWS)
        pltpu.make_async_copy(
            xg.at[block, rows_at(sec * 512, 512, 128)], feat_out.at[block], out_sem.at[0]
        ).start()
        for n in range(0, wv.shape[1], 256):
            part_sum[block, n:n + 256] = jnp.dot(
                xg[block, :], wv[:, n:n + 256], preferred_element_type=jnp.float32
            )

    def decode(at, chunk, cols):
        count = landed[at, cols].astype(jnp.int32).astype(jnp.float32)
        return count * unit_landed[chunk, :, cols]

    def encode(at, chunk, add):
        for n in range(0, part_sum.shape[1], 256):
            cols = slice(n, n + 256)
            value = part_sum[at, cols]
            if add:
                value = value + decode(at, chunk, cols)
            most = jnp.max(jnp.abs(value), axis=0, keepdims=True)
            most = jnp.maximum(most, 1e-30)
            unit_sent[chunk, :, cols] = most * (1.0 / STEPS)
            count = jnp.round(value * (STEPS / most)).astype(jnp.int32)
            sent[at, cols] = count.astype(jnp.int16)

    def finish(start, slot, a, chunk):
        def some(t, carry):
            at = rows_at(start + t * 16, 16, 16)
            hidden = part_sum[at, :] + decode(at, chunk, slice(None))
            gate = jax.nn.sigmoid(hidden)
            term = hidden * gate * read_ref[...]
            folded = term[:, 0:128]
            for n in range(128, term.shape[1], 128):
                folded = folded + term[:, n:n + 128]
            lanes[rows_at(a * SUB + t * 16, 16, 16), :] = folded

            @pl.when(sec == LAST)
            def _():
                slope[at, :] = (
                    read_ref[...] * gate * (1.0 + hidden * (1.0 - gate))
                ).astype(jnp.bfloat16)

            return carry

        lax.fori_loop(0, SUB // 16, some, 0)
        if a == 1:
            score_rows[pl.ds(slot, 1), :] = jnp.sum(
                jnp.transpose(lanes[...]), axis=0, keepdims=True
            )

    def add_up(i, half, a):
        hop = d if half == 1 else LAST - d
        onward = d + 1 if half == 1 else d - 1
        slot = i - hop
        start = slot * ROWS + half * HALF + a * SUB

        @pl.when((slot >= 0) & (slot < SLOTS))
        def _():
            at = rows_at(start, SUB, SUB)
            count = slot * 2 + a
            chunk = slot * 4 + half * 2 + a

            @pl.when(hop > 0)
            def _():
                wait_for(landed.at[at], sum_recv.at[half, count])
                wait_for(unit_landed.at[chunk], unit_recv.at[half, count])

            @pl.when(hop == 0)
            def _():
                encode(at, chunk, False)

            @pl.when((hop > 0) & (hop < LAST))
            def _():
                encode(at, chunk, True)

            @pl.when(hop < LAST)
            def _():
                push(
                    sent.at[at], landed.at[at], sum_send.at[half],
                    sum_recv.at[half, count], d_=onward,
                )
                push(
                    unit_sent.at[chunk], unit_landed.at[chunk], unit_send.at[half],
                    unit_recv.at[half, count], d_=onward,
                )

            @pl.when(hop == LAST)
            def _():
                finish(start, slot, a, chunk)

    def quarter(slot, half, q):
        return slope.at[rows_at(slot * ROWS + half * HALF + q * PIECE, PIECE, PIECE)]

    def in_range(slot):
        return (slot >= 0) & (slot < SLOTS)

    def hand_on(i, half):
        hop = d if half == 0 else LAST - d
        onward = d + 1 if half == 0 else d - 1
        source = (hop == 0) & (sec == LAST)
        no_right = (hop == 0) & (sec == LAST - 1)
        no_left = (hop == 0) & (sec == 0)

        fresh = i - 3

        @pl.when(source & in_range(fresh))
        def _():
            for q in range(LAST):
                push(
                    quarter(fresh, half, q), quarter(fresh, half, q),
                    scat_send.at[half], scat_recv.at[half, fresh], sec_=q,
                )

        slot = i - 4 - hop

        @pl.when(in_range(slot))
        def _():
            held = quarter(slot, half, sec)

            @pl.when((hop == 0) & (sec < LAST))
            def _():
                wait_for(held, scat_recv.at[half, slot])

            @pl.when(hop > 0)
            def _():
                wait_for(held, line_recv.at[half, slot])

            @pl.when(hop < LAST)
            def _():
                push(held, held, line_send.at[half], line_recv.at[half, slot], d_=onward)

            @pl.when(jnp.logical_not(no_right))
            def _():
                push(held, held, ring_send.at[half], ring_recv.at[half, slot, 0], sec_=right)

            @pl.when(jnp.logical_not(no_left))
            def _():
                push(held, held, ring_send.at[half], ring_recv.at[half, slot, 1], sec_=left)

        slot1 = i - 5 - hop

        @pl.when(in_range(slot1))
        def _():
            from_left = quarter(slot1, half, left)
            from_right = quarter(slot1, half, right)

            @pl.when(jnp.logical_not(source))
            def _():
                wait_for(from_left, ring_recv.at[half, slot1, 0])
                wait_for(from_right, ring_recv.at[half, slot1, 1])

            if half == 0:
                @pl.when(jnp.logical_not(no_right))
                def _():
                    push(
                        from_left, from_left, ring_send.at[half],
                        ring_recv.at[half, slot1, 2], sec_=right,
                    )
            else:
                @pl.when(jnp.logical_not(no_left))
                def _():
                    push(
                        from_right, from_right, ring_send.at[half],
                        ring_recv.at[half, slot1, 2], sec_=left,
                    )

        slot2 = i - 6 - hop

        @pl.when(in_range(slot2))
        def _():
            @pl.when(jnp.logical_not(source))
            def _():
                wait_for(quarter(slot2, half, origin[3]), ring_recv.at[half, slot2, 2])

            at = rows_at(slot2 * ROWS + half * HALF, HALF, HALF)
            pltpu.make_async_copy(slope.at[at], slope_out.at[at], out_sem.at[1]).start()

    is_end = (d == 0) | (d == LAST)
    which = d // LAST

    def share_terms():
        for slot in range(SLOTS):
            row = ring(y, Y_OFF[slot]) * 2 + lax.rem(h + H_OFF[slot], 2)
            mine[pl.ds(row, 1), :] = score_rows[slot:slot + 1, :]
        for k in range(1, 16):
            push(mine, peers.at[tp], peer_send, peer_recv, tp_=lax.rem(tp + k, 16))
        peers[tp] = mine[...]

    def share_scores():
        wait_for(scores_like_peers(15), peer_recv)
        summed = peers[0]
        for k in range(1, 16):
            summed = summed + peers[k]
        total[...] = summed
        for k in range(1, 16):
            push(
                total, scores.at[sec * 2 + which], score_send, score_recv,
                sec_=ring(sec, k // 4), d_=ring(d, k % 4),
            )
        scores[sec * 2 + which] = summed

    def scores_like_peers(n):
        return peers.at[0:n]

    def step(i, carry):
        @pl.when(i < SLOTS)
        def _():
            project(i)

        for a in range(2):
            add_up(i, 1, a)
            add_up(i, 0, a)

        @pl.when(i == 0)
        def _():
            second_block()

        @pl.when((i >= 1) & (i < SLOTS - 1))
        def _():
            later_block(i + 1)

        @pl.when((i == 10) & is_end)
        def _():
            share_terms()

        hand_on(i, 0)
        hand_on(i, 1)

        @pl.when((i == 12) & is_end)
        def _():
            share_scores()

        return carry

    lax.fori_loop(0, SLOTS + 9, step, 0)

    @pl.when(is_end)
    def _():
        wait_for(scores.at[0:7], score_recv)

    @pl.when(jnp.logical_not(is_end))
    def _():
        wait_for(scores.at[0:8], score_recv)

    score_ref[...] = scores[...]

    wait_for(xg.at[0:63 * PIECE], gather_send)
    for half in range(2):
        sum_hop = d if half == 1 else LAST - d
        hop = d if half == 0 else LAST - d
        source = (hop == 0) & (sec == LAST)
        one = (hop == 0) & (sec == (LAST - 1 if half == 0 else 0))
        two = (hop == 0) & (sec == (0 if half == 0 else LAST - 1))

        @pl.when(sum_hop < LAST)
        def _():
            wait_for(sent.at[0:SLOTS * HALF], sum_send.at[half])
            wait_for(unit_sent.at[0:SLOTS * 2], unit_send.at[half])

        @pl.when(source)
        def _():
            wait_for(slope.at[0:3 * SLOTS * PIECE], scat_send.at[half])

        @pl.when(hop < LAST)
        def _():
            wait_for(slope.at[0:SLOTS * PIECE], line_send.at[half])

        @pl.when(one)
        def _():
            wait_for(slope.at[0:SLOTS * PIECE], ring_send.at[half])

        @pl.when(two)
        def _():
            wait_for(slope.at[0:2 * SLOTS * PIECE], ring_send.at[half])

        @pl.when(jnp.logical_not(one | two))
        def _():
            wait_for(slope.at[0:3 * SLOTS * PIECE], ring_send.at[half])

    @pl.when(is_end)
    def _():
        wait_for(scores_like_peers(15), peer_send)
        wait_for(scores_like_peers(15), score_send)

    wait_for(feat_out, out_sem.at[0])
    wait_for(slope_out, out_sem.at[1])


def score_and_slope(responses, weights, readout):
    tokens, width, units = ROWS * SLOTS, weights.shape[1], weights.shape[2]
    block_width = width // RING
    dma = pltpu.SemaphoreType.DMA
    any_space = pl.BlockSpec(memory_space=pl.ANY)
    in_vmem = pl.BlockSpec(memory_space=pltpu.VMEM)
    return pl.pallas_call(
        slab_kernel,
        out_shape=(
            jax.ShapeDtypeStruct((8, 8, 128), jnp.float32),
            jax.ShapeDtypeStruct((tokens, units), jnp.bfloat16),
            jax.ShapeDtypeStruct((tokens, block_width), jnp.bfloat16),
        ),
        in_specs=[any_space, any_space, in_vmem],
        out_specs=(in_vmem, any_space, any_space),
        scratch_shapes=[
            pltpu.VMEM((tokens, width), jnp.bfloat16),
            pltpu.VMEM((width, units), jnp.bfloat16),
            pltpu.VMEM((tokens, units), jnp.float32),
            pltpu.VMEM((tokens, units), jnp.int16),
            pltpu.VMEM((tokens, units), jnp.int16),
            pltpu.VMEM((4 * SLOTS, 1, units), jnp.float32),
            pltpu.VMEM((4 * SLOTS, 1, units), jnp.float32),
            pltpu.VMEM((tokens, units), jnp.bfloat16),
            pltpu.VMEM((128, 128), jnp.float32),
            pltpu.VMEM((8, 128), jnp.float32),
            pltpu.VMEM((8, 128), jnp.float32),
            pltpu.VMEM((16, 8, 128), jnp.float32),
            pltpu.VMEM((8, 128), jnp.float32),
            pltpu.VMEM((8, 8, 128), jnp.float32),
            dma((2,)), dma((2,)), dma, dma, dma((2, 3)), dma((8, 4)), dma((8, 4)),
            dma((2,)), dma((2, 16)), dma((2,)), dma((2, 16)), dma((2,)), dma((2, 8)), dma((2,)), dma((2, 8)),
            dma((2,)), dma((2, 8, 3)), dma, dma, dma, dma,
        ],
        compiler_params=pltpu.CompilerParams(
            collective_id=0, has_side_effects=True, vmem_limit_bytes=50 * 1024 * 1024,
        ),
        name="score_and_slope",
    )(responses, weights, readout)


def advantages(rewards, groups):
    same_group = (groups[:, None] == groups[None, :]).astype(jnp.float32)
    members = jnp.sum(same_group, axis=1)
    group_mean = jnp.sum(same_group * rewards[None, :], axis=1) / members
    spread = jnp.sum(same_group * (rewards[None, :] - group_mean[:, None]) ** 2, axis=1) / members
    return (rewards - group_mean) / jnp.sqrt(spread + 1.0)


def contract_rows(left, right):
    return lax.dot_general(
        left, right, (((0,), (0,)), ((), ())), preferred_element_type=jnp.float32
    )


def local(responses, weights, readout, lengths, groups):
    scores, slope, features = score_and_slope(responses, weights, readout)
    total_rows = slope.shape[0]
    resp_count = lengths.shape[0]
    joined = scores.reshape(RING, total_rows)
    shape = (2, 4, 2, 2, SUB)
    half, at_y, at_h, at_x, inner = (
        lax.broadcasted_iota(jnp.int32, shape, n) for n in range(5)
    )
    position = (((half * 2 + at_x) * 4 + at_y) * 2 + at_h) * SUB + inner
    position = position.reshape(total_rows)
    starts = jnp.cumsum(lengths) - lengths
    finish = starts + lengths
    in_response = (
        (position[:, None] >= starts[None, :]) & (position[:, None] < finish[None, :])
    ).astype(jnp.float32)
    last_token = (position[:, None] == finish[None, :] - 1).astype(jnp.float32)
    token_len = jnp.sum(in_response * lengths.astype(jnp.float32)[None, :], axis=1)
    lp_old = jax.nn.log_sigmoid(joined[0])
    lp_ref = jax.nn.log_sigmoid(joined[1])
    lp_new = jax.nn.log_sigmoid(joined[3])
    prob_ratio = jnp.exp(lp_new - lp_old)
    log_gap = lp_ref - lp_new
    penalty = kl_weight * (jnp.exp(log_gap) - log_gap - 1.0)
    rewards = jnp.sum(last_token * joined[2][:, None], axis=0)
    advantage = advantages(rewards, groups)
    token_adv = jnp.sum(in_response * advantage[None, :], axis=1)
    token_loss = -prob_ratio * token_adv + penalty
    policy_loss = jnp.sum(token_loss / token_len) / resp_count
    coeff = (
        total_rows
        / (resp_count * token_len)
        * (-prob_ratio * token_adv + kl_weight * (1.0 - jnp.exp(log_gap)))
        * jax.nn.sigmoid(-joined[3])
    )
    tp = lax.axis_index("tp")
    block = (
        lax.rem(tp // 4 + jnp.array(Y_OFF, jnp.int32), 4) * 2
        + lax.rem(tp // 2 + jnp.array(H_OFF, jnp.int32), 2)
    )
    by_block = coeff.reshape(2, SLOTS, HALF).transpose(1, 0, 2).reshape(SLOTS, ROWS)
    ordered = jnp.take(by_block, block, axis=0).reshape(total_rows)
    hidden_grad = (ordered[:, None] * slope.astype(jnp.float32)).astype(jnp.bfloat16)
    weight_grad = contract_rows(features, hidden_grad)
    return (weight_grad.astype(jnp.bfloat16)[None], policy_loss)


def solution(mesh):
    return jax.shard_map(
        local,
        mesh=mesh,
        in_specs=(
            P(("section", "tp"), "dp"),
            P("section", "dp", "tp"),
            P("section", "tp"),
            P(),
            P(),
        ),
        out_specs=(P("dp", "section", "tp"), P()),
        check_vma=False,
    )
```
